32 devices in a mesh: row: 2 (over y), col: 16 (over z, x, core).
Axes of the slice: x: 2, y: 2, z: 4, core: 2. Of those that a mesh axis runs over, the one named last changes fastest.
Arguments:
- object_field: float32 [2, 512, 4096], P(None, 'row', 'col'), may hold values from -6 to 6
- probe_field: float32 [2, 256, 256], replicated, may hold values from -4.2 to 4.2
- amplitudes: bfloat16 [2, 16, 6, 256, 256], P('row', 'col'), may hold values from 0 to 2
- offsets: int32 [2, 16, 6, 2], P('row', 'col'), may hold values from 0 to 256
- counts: int32 [2, 16], P('row', 'col'), may hold values from 2 to 6
Outputs:
- updated_object: float32 [2, 512, 4096], P(None, 'row', 'col')
The draws below stay inside these ranges and needn't reach their ends.
Inputs may be any that keep to these rules, and one draw needn't show every extreme that they name: offsets[r, c, k] places slot k of tile (r, c) as stated in the reference program, so a patch reaches at most 128 pixels beyond its tile. Tile (r, c) uses slots 0 to counts[r, c] - 1; offsets and amplitudes of the other slots are ignored.
All inputs are finite; a program needn't handle non-finite values.
Results may differ from the reference program's by a relative error of at most 0.0021.
Values sent between devices are 32-bit elements; how exact they have to be, the bound alone decides.
A program may use at most 64 MiB of HBM per device.

```python
import math
import jax
import jax.numpy as jnp
from jax import lax

TILE = 256
RIM = 128
MAXPOS = 6
ITERS = 2
TILES_R = 2
TILES_C = 16


def place_ends(entries, key, low, top_value):
    longest = entries.shape.index(max(entries.shape))
    spots = []
    for shift in (0, 1):
        where = [jax.random.randint(jax.random.fold_in(key, axis), (), 0, length) for axis, length in enumerate(entries.shape)]
        where[longest] = (where[longest] + shift) % entries.shape[longest]
        spots.append(tuple(where))
    return entries.at[spots[0]].set(low).at[spots[1]].set(top_value)


def steps_of(key, dims, split, least, high):
    loudness = 1.0
    for axis_at, parts in split:
        steps = jax.random.uniform(jax.random.fold_in(jax.random.fold_in(key, 6), axis_at), (parts,), jnp.float32, least / len(split), high / len(split))
        loudness = loudness * jnp.repeat(jnp.exp(steps), dims[axis_at] // parts).reshape((-1,) + (1,) * (len(dims) - 1 - axis_at))
    return loudness


def bell_draw(own_key, extent, scale, limit, cuts=(), kind=jnp.bfloat16):
    factor_of = steps_of(own_key, extent, cuts, -0.22, 0.18) if cuts else 1.0
    drawn = jax.random.normal(own_key, extent, jnp.float32) * scale * factor_of
    return jnp.minimum(jnp.maximum(drawn, -limit), limit).astype(kind)


def setup_inputs(seed: int = 0) -> dict:
    arg_keys = jax.random.split(jax.random.key(seed), 6)
    return {
        "object_field": bell_draw(arg_keys[0], (2, TILES_R * TILE, TILES_C * TILE), 1.0, 6.0, ((1, 2), (2, 16)), jnp.float32),
        "probe_field": bell_draw(arg_keys[1], (2, TILE, TILE), 0.7, 4.2, (), jnp.float32),
        "amplitudes": jnp.clip(2.0 * jax.random.uniform(arg_keys[2], (TILES_R, TILES_C, MAXPOS, TILE, TILE), jnp.float32) ** steps_of(arg_keys[2], (TILES_R, TILES_C, MAXPOS, TILE, TILE), ((0, 2), (1, 16)), -0.2, 0.2), 0.0, 2.0).astype(jnp.bfloat16),
        "offsets": place_ends(jax.random.randint(arg_keys[3], (TILES_R, TILES_C, MAXPOS, 2), 0, TILE + 1), jax.random.fold_in(arg_keys[3], 1), 0, TILE).astype(jnp.int32),
        "counts": place_ends(jax.random.randint(arg_keys[4], (TILES_R, TILES_C), 2, MAXPOS + 1), jax.random.fold_in(arg_keys[4], 1), 2, MAXPOS).astype(jnp.int32),
    }


smooth_term = 0.25
step_size = 0.5
regular_term = 1.0

def dft_table(length):
    positions = jnp.arange(length, dtype=jnp.int32)
    phase_step = positions[:, None] * positions[None, :] % length
    phase_angle = phase_step.astype(jnp.float32) * (2.0 * math.pi / length)
    norm_scale = 1.0 / math.sqrt(length)
    cosine = jnp.cos(phase_angle) * norm_scale
    sine_part = jnp.sin(phase_angle) * norm_scale
    return jnp.stack([jnp.stack([cosine, sine_part]), jnp.stack([-sine_part, cosine])]).astype(jnp.bfloat16)

def transform(field, matrices, inverse):
    if inverse:
        first_form = 'pqab,spbc->sqac'
        second_form = 'spab,pqbc->sqac'
    else:
        first_form = 'qpab,spbc->sqac'
        second_form = 'spab,qpbc->sqac'
    wide_table = matrices.astype(jnp.float32)
    half_done = jnp.einsum(first_form, wide_table, field.astype(jnp.float32), precision=lax.Precision.HIGHEST).astype(jnp.bfloat16)
    return jnp.einsum(second_form, half_done.astype(jnp.float32), wide_table, precision=lax.Precision.HIGHEST)

def patch_gradients(patches, probe_field, amplitudes, in_use, matrices):
    probe_real = probe_field[0]
    probe_imag = probe_field[1]
    object_real = patches[:, 0]
    object_imag = patches[:, 1]
    exit_wave = jnp.stack([probe_real * object_real - probe_imag * object_imag, probe_real * object_imag + probe_imag * object_real], axis=1).astype(jnp.bfloat16)
    spectrum = transform(exit_wave, matrices, False)
    modulus = jnp.sqrt(spectrum[:, 0] * spectrum[:, 0] + spectrum[:, 1] * spectrum[:, 1] + smooth_term)
    factor = (1.0 - amplitudes.astype(jnp.float32) / modulus) * in_use[:, None, None]
    residual = (spectrum * factor[:, None]).astype(jnp.bfloat16)
    back_wave = transform(residual, matrices, True)
    return jnp.stack([probe_real * back_wave[:, 0] + probe_imag * back_wave[:, 1], probe_real * back_wave[:, 1] - probe_imag * back_wave[:, 0]], axis=1)

def reference(object_field, probe_field, amplitudes, offsets, counts):
    matrices = dft_table(TILE)
    tile_total = TILES_R * TILES_C
    flat_offsets = offsets.reshape(tile_total, MAXPOS, 2)
    flat_counts = counts.reshape(tile_total)
    flat_amps = amplitudes.reshape(tile_total, MAXPOS, TILE, TILE)
    slot_index = jnp.arange(MAXPOS, dtype=jnp.int32)
    probe_power = probe_field[0] * probe_field[0] + probe_field[1] * probe_field[1]
    padded_rows = TILES_R * TILE + 2 * RIM
    padded_cols = TILES_C * TILE + 2 * RIM
    zero_index = jnp.zeros((), jnp.int32)
    tile_ids = jnp.arange(tile_total, dtype=jnp.int32)

    def corners(tile_id):
        tile_row = tile_id // TILES_C
        tile_col = tile_id % TILES_C
        top_rows = (tile_row * TILE + flat_offsets[tile_id, :, 0]).astype(jnp.int32)
        left_cols = (tile_col * TILE + flat_offsets[tile_id, :, 1]).astype(jnp.int32)
        in_use = (slot_index < flat_counts[tile_id]).astype(jnp.float32)
        return (top_rows, left_cols, in_use)

    def light_step(grid, tile_id):
        top_rows, left_cols, in_use = corners(tile_id)

        def add_light(slot, inner):
            window = lax.dynamic_slice(inner, (top_rows[slot], left_cols[slot]), (TILE, TILE))
            return lax.dynamic_update_slice(inner, window + probe_power * in_use[slot], (top_rows[slot], left_cols[slot]))
        return (lax.fori_loop(0, MAXPOS, add_light, grid), None)
    light_grid, leftover = lax.scan(light_step, jnp.zeros((padded_rows, padded_cols), jnp.float32), tile_ids)
    illumination = light_grid[RIM:RIM + TILES_R * TILE, RIM:RIM + TILES_C * TILE]
    for iteration in range(ITERS):
        padded_object = jnp.pad(object_field, ((0, 0), (RIM, RIM), (RIM, RIM)))

        def grad_step(grid, tile_id):
            top_rows, left_cols, in_use = corners(tile_id)

            def cut_patch(top_row, left_col):
                return lax.dynamic_slice(padded_object, (zero_index, top_row, left_col), (2, TILE, TILE))
            patches = jax.vmap(cut_patch)(top_rows, left_cols)
            pieces = patch_gradients(patches, probe_field, flat_amps[tile_id], in_use, matrices)

            def add_piece(slot, inner):
                where_to = (zero_index, top_rows[slot], left_cols[slot])
                window = lax.dynamic_slice(inner, where_to, (2, TILE, TILE))
                return lax.dynamic_update_slice(inner, window + pieces[slot], where_to)
            return (lax.fori_loop(0, MAXPOS, add_piece, grid), None)
        grad_grid, leftover = lax.scan(grad_step, jnp.zeros((2, padded_rows, padded_cols), jnp.float32), tile_ids)
        gradient = grad_grid[:, RIM:RIM + TILES_R * TILE, RIM:RIM + TILES_C * TILE]
        object_field = object_field - step_size * gradient / (illumination + regular_term)
    return object_field
```

```python
import functools
import math

import jax
import jax.numpy as jnp
import numpy as np
from jax import lax
from jax.experimental import pallas as pl
from jax.experimental.pallas import tpu as pltpu
from jax.sharding import PartitionSpec as P

TILE = 256
RIM = 128
MAXPOS = 6
ITERS = 2
LANES = 128
HALF = 128
CHUNK = 32
VMEM_LIMIT = 28 * 1024 * 1024
WIRE_COST = pl.CostEstimate(flops=0, transcendentals=0, bytes_accessed=40_000_000)

smooth_term = 0.25
step_size = 0.5
regular_term = 1.0

AXES = ("row", "col")
SIDES = [(-1, 0), (1, 0), (0, -1), (0, 1), (-1, -1), (-1, 1), (1, -1), (1, 1)]
CORNERS = SIDES[4:]


def dft_tables():
    positions = np.arange(TILE)
    phase_step = (positions[:, None] * positions[None, :]) % TILE
    angle = phase_step.astype(np.float32) * np.float32(2.0 * math.pi / TILE)
    scale = np.float32(1.0 / math.sqrt(TILE))
    real = np.cos(angle).astype(np.float32) * scale
    imag = -np.sin(angle).astype(np.float32) * scale
    left, right = [], []
    for parity in range(2):
        r = real[parity::2, :HALF]
        i = imag[parity::2, :HALF]
        m = np.block([[r, -i], [i, r]])
        left.append(m)
        right.append(m.T)
    return np.stack(left + right).astype(jnp.bfloat16)


def order_table():
    picked = np.concatenate([np.arange(0, TILE, 2), np.arange(1, TILE, 2)])
    table = np.zeros((TILE, TILE), np.float32)
    table[np.arange(TILE), picked] = 1.0
    return np.stack([table, table.T]).astype(jnp.bfloat16)


def edge(step, length):
    if step < 0:
        return slice(0, RIM)
    if step > 0:
        return slice(length - RIM, length)
    return slice(0, length)


def zone(step):
    return (slice(0, RIM), slice(RIM, RIM + TILE), slice(RIM + TILE, 2 * RIM + TILE))[step + 1]


def rim_block(right):
    return 0 if right < 0 else 3


def own_block(right):
    return 1 if right < 0 else 2


def inside(row, col):
    rows, cols = lax.axis_size("row"), lax.axis_size("col")
    return (row >= 0) & (row < rows) & (col >= 0) & (col < cols)


def greet(row, col):
    barrier = pltpu.get_barrier_semaphore()
    peers = 0
    for down, right in SIDES[:4]:
        present = inside(row + down, col + right)
        peers = peers + jnp.where(present, 1, 0)

        @pl.when(present)
        def _():
            pl.semaphore_signal(
                barrier,
                inc=1,
                device_id=(row + down, col + right),
                device_id_type=pl.DeviceIdType.MESH,
            )

    pl.semaphore_wait(barrier, peers)


def transfer(source, landing, sends, receives, slot, device):
    return pltpu.make_async_remote_copy(
        src_ref=source,
        dst_ref=landing,
        send_sem=sends.at[slot],
        recv_sem=receives.at[slot],
        device_id=device,
        device_id_type=pl.DeviceIdType.MESH,
    )


def half_slot(down, right):
    return (0 if down < 0 else 1) + (0 if right < 0 else 8)


def halo_copies(source, ext, sends, receives):
    def row_copy(down, right, device):
        return transfer(
            source(down, right),
            ext.at[:, own_block(right), zone(-down), :],
            sends,
            receives,
            half_slot(down, right),
            device,
        )

    def col_copy(right, device):
        at = SIDES.index((0, right))
        return transfer(
            source(0, right),
            ext.at[:, rim_block(-right), zone(0), :],
            sends,
            receives,
            at,
            device,
        )

    def corner_copy(down, right, device):
        at = SIDES.index((down, right))
        return transfer(
            ext.at[:, own_block(right), zone(-down), :],
            ext.at[:, rim_block(-right), zone(-down), :],
            sends,
            receives,
            at,
            device,
        )

    return row_copy, col_copy, corner_copy


def halo_begin(copies, row, col):
    row_copy, col_copy, _ = copies
    for down, right in CORNERS:

        @pl.when(inside(row + down, col))
        def _():
            row_copy(down, right, (row + down, col)).start()

    for right in (-1, 1):

        @pl.when(inside(row, col + right))
        def _():
            col_copy(right, (row, col + right)).start()


def blank_outside(ext, row, col):
    for down, right in SIDES:

        @pl.when(jnp.logical_not(inside(row - down, col - right)))
        def _():
            blocks = slice(1, 3) if right == 0 else slice(rim_block(-right), rim_block(-right) + 1)
            part = ext.at[:, blocks, zone(-down), :]
            part[...] = jnp.zeros(part.shape, jnp.float32)


def halo_finish(copies, row, col):
    row_copy, col_copy, corner_copy = copies
    for down, right in CORNERS:

        @pl.when(inside(row - down, col))
        def _():
            row_copy(down, right, (row - down, col)).wait_recv()

        @pl.when(inside(row - down, col) & inside(row, col + right))
        def _():
            corner_copy(down, right, (row, col + right)).start()

    for right in (-1, 1):

        @pl.when(inside(row, col - right))
        def _():
            col_copy(right, (row, col - right)).wait_recv()

    for down, right in CORNERS:

        @pl.when(inside(row - down, col - right))
        def _():
            corner_copy(down, right, (row, col - right)).wait_recv()

    for down, right in CORNERS:

        @pl.when(inside(row + down, col))
        def _():
            row_copy(down, right, (row + down, col)).wait_send()

        @pl.when(inside(row - down, col) & inside(row, col + right))
        def _():
            corner_copy(down, right, (row, col + right)).wait_send()

    for right in (-1, 1):

        @pl.when(inside(row, col + right))
        def _():
            col_copy(right, (row, col + right)).wait_send()


def prepare(offs, probe, amps, order, turned, sorted_amps, swap):
    lane = lax.broadcasted_iota(jnp.int32, (CHUNK, LANES), 1)

    def one_slot(slot, carry):
        left = offs[1, slot] % TILE
        shift = left % LANES
        low = jnp.where(lane >= shift, 1, 0)
        straight = low != left // LANES
        for p in range(2):
            for at in range(0, TILE, CHUNK):
                rows = slice(at, at + CHUNK)
                a = pltpu.roll(probe[p, rows, :LANES], shift, 1)
                b = pltpu.roll(probe[p, rows, LANES:], shift, 1)
                turned[slot, p, 0, rows, :] = jnp.where(straight, a, b)
                turned[slot, p, 1, rows, :] = jnp.where(straight, b, a)
        swap[...] = jnp.dot(order[0], amps[slot], preferred_element_type=jnp.float32).astype(jnp.bfloat16)
        placed = jnp.dot(swap[...], order[1], preferred_element_type=jnp.float32).astype(jnp.bfloat16)
        sorted_amps[slot, 0] = placed[:, :LANES]
        sorted_amps[slot, 1] = placed[:, LANES:]
        return carry

    lax.fori_loop(0, MAXPOS, one_slot, 0)


def halo_kernel(offs, field, probe, amps, order, ext, turned, sorted_amps, swap, sends, receives):
    row, col = lax.axis_index("row"), lax.axis_index("col")
    greet(row, col)

    def source(down, right):
        cols = slice(0, LANES) if right < 0 else slice(LANES, 2 * LANES)
        return field.at[:, edge(down, TILE), cols]

    copies = halo_copies(source, ext, sends, receives)
    halo_begin(copies, row, col)
    blank_outside(ext, row, col)
    for block in range(2):
        ext[:, 1 + block, RIM : RIM + TILE, :] = field[:, :, block * LANES : (block + 1) * LANES]
    prepare(offs, probe, amps, order, turned, sorted_amps, swap)
    halo_finish(copies, row, col)


def gradient_kernel(planes, offs, cnt, ext, turned, amps, mats, canvas, *scratch):
    canvas[...] = jnp.zeros_like(canvas)
    lane = lax.broadcasted_iota(jnp.int32, (CHUNK, LANES), 1)
    bf16 = jnp.bfloat16

    def product(a, b):
        return jnp.dot(a, b, preferred_element_type=jnp.float32)

    def stages(slot, used, buffers):
        waves, halves, spectra = buffers
        top = offs[0, slot]
        left = offs[1, slot]
        near = [lane >= left - b * LANES for b in range(2)]

        def gather():
            for at in range(0, HALF, CHUNK):
                for b in range(2):
                    cols = slice(b * LANES, (b + 1) * LANES)
                    parts = []
                    for far in (0, HALF):
                        rows = pl.ds(top + at + far, CHUNK)
                        wr, wi = [
                            jnp.where(near[b], ext[p, b, rows, :], ext[p, b + 2, rows, :])
                            for p in range(2)
                        ]
                        pr = turned[slot, 0, b, at + far : at + far + CHUNK, :]
                        pi = turned[slot, 1, b, at + far : at + far + CHUNK, :]
                        parts.append((pr * wr - pi * wi, pr * wi + pi * wr))
                    for p in range(2):
                        rows = slice(p * HALF + at, p * HALF + at + CHUNK)
                        waves[0, rows, cols] = (parts[0][p] + parts[1][p]).astype(bf16)
                        waves[1, rows, cols] = (parts[0][p] - parts[1][p]).astype(bf16)

        def forward_rows():
            for parity in range(2):
                y = product(mats[parity], waves[parity])
                a, b = y[:, :LANES], y[:, LANES:]
                rows = slice(parity * HALF, (parity + 1) * HALF)
                for at, z in enumerate((a + b, a - b)):
                    halves[at, rows, :LANES] = z[:HALF].astype(bf16)
                    halves[at, rows, LANES:] = z[HALF:].astype(bf16)

        def forward_cols():
            for parity in range(2):
                spectra[parity] = product(halves[parity], mats[2 + parity])

        def residual():
            for parity in range(2):
                for at in range(0, TILE, CHUNK):
                    sr = spectra[parity, at : at + CHUNK, :LANES]
                    si = spectra[parity, at : at + CHUNK, LANES:]
                    amp = amps[slot, parity, at : at + CHUNK, :].astype(jnp.float32)
                    factor = 1.0 - amp * lax.rsqrt(sr * sr + si * si + smooth_term)
                    if used is not None:
                        factor = jnp.where(used, factor, 0.0)
                    odd, inner = divmod(at, HALF)
                    cols = slice(parity * LANES, (parity + 1) * LANES)
                    waves[odd, inner : inner + CHUNK, cols] = (sr * factor).astype(bf16)
                    waves[odd, HALF + inner : HALF + inner + CHUNK, cols] = (si * factor).astype(bf16)

        def back_rows():
            e = product(mats[2], waves[0])
            o = product(mats[3], waves[1])
            for at, z in enumerate((e + o, e - o)):
                rows = slice(at * HALF, (at + 1) * HALF)
                for parity in range(2):
                    cols = slice(parity * LANES, (parity + 1) * LANES)
                    halves[parity, rows, :LANES] = z[:HALF, cols].astype(bf16)
                    halves[parity, rows, LANES:] = z[HALF:, cols].astype(bf16)

        def back_cols():
            for parity in range(2):
                spectra[parity] = product(halves[parity], mats[parity])

        def scatter():
            for at in range(0, TILE, CHUNK):
                rows = pl.ds(top + at, CHUNK)
                er, ei = [spectra[0, at : at + CHUNK, p * LANES : (p + 1) * LANES] for p in range(2)]
                pr_, pi_ = [spectra[1, at : at + CHUNK, p * LANES : (p + 1) * LANES] for p in range(2)]
                for b in range(2):
                    br, bi = (er + pr_, ei + pi_) if b == 0 else (er - pr_, ei - pi_)
                    pr = turned[slot, 0, b, at : at + CHUNK, :]
                    pi = turned[slot, 1, b, at : at + CHUNK, :]
                    pieces = [pr * br + pi * bi, pr * bi - pi * br]
                    if planes > 2:
                        light = pr * pr + pi * pi
                        pieces.append(light if used is None else jnp.where(used, light, 0.0))
                    for p, piece in enumerate(pieces):
                        canvas[p, b, rows, :] += jnp.where(near[b], piece, 0.0)
                        canvas[p, b + 2, rows, :] += jnp.where(near[b], 0.0, piece)

        return [gather, forward_rows, forward_cols, residual, back_rows, back_cols, scatter]

    first, second = scratch[:3], scratch[3:]

    def two_slots(pair, carry):
        a = stages(2 * pair, None, first)
        b = stages(2 * pair + 1, 2 * pair + 1 < cnt[0], second)
        a[0]()
        for at in range(1, len(a)):
            a[at]()
            b[at - 1]()
        b[-1]()
        return carry

    lax.fori_loop(0, (cnt[0] + 1) // 2, two_slots, 0)


def update_kernel(first, canvas, ext, *refs):
    if first:
        new, scale_out = refs[:2]
        halo_sems = refs[-2:]
        refs = refs[2:-2]
    else:
        scale_in, new = refs[:2]
        refs = refs[2:]
    land_corner, land_col, land_row, total, sends, receives = refs
    row, col = lax.axis_index("row"), lax.axis_index("col")
    greet(row, col)

    def corner_copy(down, right, device):
        at = SIDES.index((down, right))
        return transfer(
            canvas.at[:, rim_block(right), zone(down), :],
            land_corner.at[at - 4],
            sends,
            receives,
            at,
            device,
        )

    def col_copy(right, device):
        at = SIDES.index((0, right))
        return transfer(
            canvas.at[:, rim_block(right), zone(0), :], land_col.at[at - 2], sends, receives, at, device
        )

    def row_copy(down, right, device):
        vertical = 0 if down < 0 else 1
        return transfer(
            total.at[:, own_block(right) - 1, zone(down), :],
            land_row.at[vertical, :, own_block(right) - 1],
            sends,
            receives,
            half_slot(down, right),
            device,
        )

    for down, right in CORNERS:

        @pl.when(inside(row + down, col + right))
        def _():
            corner_copy(down, right, (row, col + right)).start()

    for right in (-1, 1):

        @pl.when(inside(row, col + right))
        def _():
            col_copy(right, (row, col + right)).start()

    total[...] = canvas[:, 1:3]

    def send_half(side):
        block = own_block(side) - 1
        for down in (-1, 1):

            @pl.when(inside(row + down, col) & inside(row, col + side))
            def _():
                corner_copy(down, -side, (row, col + side)).wait_recv()
                total[:, block, zone(down), :] += land_corner[SIDES.index((down, -side)) - 4]

            @pl.when(inside(row + down, col))
            def _():
                row_copy(down, side, (row + down, col)).start()

    @pl.when(col % 2 == 1)
    def _():
        send_half(-1)
        send_half(1)

    @pl.when(col % 2 == 0)
    def _():
        send_half(1)
        send_half(-1)

    for right in (-1, 1):

        @pl.when(inside(row, col - right))
        def _():
            col_copy(right, (row, col - right)).wait_recv()
            total[:, own_block(-right) - 1, zone(0), :] += land_col[SIDES.index((0, right)) - 2]

    for down, right in CORNERS:

        @pl.when(inside(row - down, col))
        def _():
            row_copy(down, right, (row - down, col)).wait_recv()
            part = slice(RIM, 2 * RIM) if down > 0 else slice(TILE, TILE + RIM)
            total[:, own_block(right) - 1, part, :] += land_row[0 if down < 0 else 1, :, own_block(right) - 1]

    for down, right in CORNERS:

        @pl.when(inside(row + down, col + right))
        def _():
            corner_copy(down, right, (row, col + right)).wait_send()

        @pl.when(inside(row + down, col))
        def _():
            row_copy(down, right, (row + down, col)).wait_send()

    for right in (-1, 1):

        @pl.when(inside(row, col + right))
        def _():
            col_copy(right, (row, col + right)).wait_send()

    for block in range(2):
        if first:
            scale = step_size / (total[2, block, zone(0), :] + regular_term)
            scale_out[block] = scale
        else:
            scale = scale_in[block]
        for p in range(2):
            value = ext[p, 1 + block, zone(0), :] - total[p, block, zone(0), :] * scale
            if first:
                new[p, 1 + block, zone(0), :] = value
            else:
                new[p, :, block * LANES : (block + 1) * LANES] = value

    if first:

        def source(down, right):
            part = {-1: slice(RIM, 2 * RIM), 0: zone(0), 1: slice(TILE, TILE + RIM)}[down]
            return new.at[:, own_block(right), part, :]

        copies = halo_copies(source, new, *halo_sems)
        halo_begin(copies, row, col)
        blank_outside(new, row, col)
        halo_finish(copies, row, col)


def vmem(count):
    return [pl.BlockSpec(memory_space=pltpu.VMEM)] * count


def smem(count):
    return [pl.BlockSpec(memory_space=pltpu.SMEM)] * count


def dma_sems():
    return [pltpu.SemaphoreType.DMA((10,))] * 2


def f32(*shape):
    return jax.ShapeDtypeStruct(shape, jnp.float32)


def wire_params(identity):
    return pltpu.CompilerParams(
        collective_id=identity, has_side_effects=True, vmem_limit_bytes=VMEM_LIMIT
    )


def gradient(planes, offs, cnt, ext, turned, amps, mats):
    slot_scratch = [
        pltpu.VMEM((2, TILE, TILE), jnp.bfloat16),
        pltpu.VMEM((2, TILE, TILE), jnp.bfloat16),
        pltpu.VMEM((2, TILE, TILE), jnp.float32),
    ]
    return pl.pallas_call(
        functools.partial(gradient_kernel, planes),
        out_shape=f32(planes, 4, 2 * TILE, LANES),
        in_specs=smem(2) + vmem(4),
        out_specs=vmem(1)[0],
        scratch_shapes=slot_scratch * 2,
        compiler_params=pltpu.CompilerParams(vmem_limit_bytes=VMEM_LIMIT),
        name=f"gradient{planes}",
    )(offs, cnt, ext, turned, amps, mats)


def halo(offs, field, probe, amps, order):
    return pl.pallas_call(
        halo_kernel,
        out_shape=[
            f32(2, 4, 2 * TILE, LANES),
            f32(MAXPOS, 2, 2, TILE, LANES),
            jax.ShapeDtypeStruct((MAXPOS, 2, TILE, LANES), jnp.bfloat16),
        ],
        in_specs=smem(1) + vmem(4),
        out_specs=vmem(3),
        scratch_shapes=[pltpu.VMEM((TILE, TILE), jnp.bfloat16)] + dma_sems(),
        compiler_params=wire_params(0),
        cost_estimate=WIRE_COST,
        name="halo",
    )(offs, field, probe, amps, order)


def update(planes, canvas, ext, scale):
    first = scale is None
    if first:
        shapes = [f32(2, 4, 2 * TILE, LANES), f32(2, TILE, LANES)]
    else:
        shapes = [f32(2, TILE, TILE)]
    operands = [canvas, ext] + ([] if first else [scale])
    return pl.pallas_call(
        functools.partial(update_kernel, first),
        out_shape=shapes,
        in_specs=vmem(len(operands)),
        out_specs=vmem(len(shapes)),
        scratch_shapes=[
            pltpu.VMEM((4, planes, HALF, LANES), jnp.float32),
            pltpu.VMEM((2, planes, TILE, LANES), jnp.float32),
            pltpu.VMEM((2, planes, 2, HALF, LANES), jnp.float32),
            pltpu.VMEM((planes, 2, 2 * TILE, LANES), jnp.float32),
        ]
        + dma_sems() * (2 if first else 1),
        compiler_params=wire_params(1 if first else 2),
        cost_estimate=WIRE_COST,
        name="exchange" if first else "finish",
    )(*operands)


def per_device(object_field, probe_field, amplitudes, offsets, counts):
    mats = jnp.asarray(dft_tables())
    order = jnp.asarray(order_table())
    offs = offsets.reshape(MAXPOS, 2).T
    cnt = counts.reshape(1)
    amps = amplitudes.reshape(MAXPOS, TILE, TILE)
    ext, turned, amps = halo(offs, object_field, probe_field, amps, order)
    scale = None
    for iteration in range(ITERS):
        planes = 3 if iteration == 0 else 2
        canvas = gradient(planes, offs, cnt, ext, turned, amps, mats)
        if iteration == 0:
            ext, scale = update(planes, canvas, ext, None)
        else:
            (field,) = update(planes, canvas, ext, scale)
    return field


def solution(mesh):
    in_specs = (
        P(None, "row", "col"),
        P(),
        P("row", "col", None, None, None),
        P("row", "col", None, None),
        P("row", "col"),
    )
    out_specs = P(None, "row", "col")
    return jax.shard_map(
        per_device, mesh=mesh, in_specs=in_specs, out_specs=out_specs, check_vma=False
    )
```

```python
import functools
import math

import jax
import jax.numpy as jnp
import numpy as np
from jax import lax
from jax.experimental import pallas as pl
from jax.experimental.pallas import tpu as pltpu
from jax.sharding import PartitionSpec as P

TILE = 256
RIM = 128
MAXPOS = 6
ITERS = 2
LANES = 128
HALF = 128
CHUNK = 32
VMEM_LIMIT = 28 * 1024 * 1024
WIRE_COST = pl.CostEstimate(flops=0, transcendentals=0, bytes_accessed=40_000_000)

smooth_term = 0.25
step_size = 0.5
regular_term = 1.0

AXES = ("row", "col")
SIDES = [(-1, 0), (1, 0), (0, -1), (0, 1), (-1, -1), (-1, 1), (1, -1), (1, 1)]
CORNERS = SIDES[4:]


def dft_tables():
    positions = np.arange(TILE)
    phase_step = (positions[:, None] * positions[None, :]) % TILE
    angle = phase_step.astype(np.float32) * np.float32(2.0 * math.pi / TILE)
    scale = np.float32(1.0 / math.sqrt(TILE))
    real = np.cos(angle).astype(np.float32) * scale
    imag = -np.sin(angle).astype(np.float32) * scale
    left, right = [], []
    for parity in range(2):
        r = real[parity::2, :HALF]
        i = imag[parity::2, :HALF]
        m = np.block([[r, -i], [i, r]])
        left.append(m)
        right.append(m.T)
    return np.stack(left + right).astype(jnp.bfloat16)


def order_table():
    picked = np.concatenate([np.arange(0, TILE, 2), np.arange(1, TILE, 2)])
    table = np.zeros((TILE, TILE), np.float32)
    table[np.arange(TILE), picked] = 1.0
    return np.stack([table, table.T]).astype(jnp.bfloat16)


def edge(step, length):
    if step < 0:
        return slice(0, RIM)
    if step > 0:
        return slice(length - RIM, length)
    return slice(0, length)


def zone(step):
    return (slice(0, RIM), slice(RIM, RIM + TILE), slice(RIM + TILE, 2 * RIM + TILE))[step + 1]


def rim_block(right):
    return 0 if right < 0 else 3


def own_block(right):
    return 1 if right < 0 else 2


def inside(row, col):
    rows, cols = lax.axis_size("row"), lax.axis_size("col")
    return (row >= 0) & (row < rows) & (col >= 0) & (col < cols)


def greet(row, col):
    barrier = pltpu.get_barrier_semaphore()
    peers = 0
    for down, right in SIDES[:4]:
        present = inside(row + down, col + right)
        peers = peers + jnp.where(present, 1, 0)

        @pl.when(present)
        def _():
            pl.semaphore_signal(
                barrier,
                inc=1,
                device_id=(row + down, col + right),
                device_id_type=pl.DeviceIdType.MESH,
            )

    pl.semaphore_wait(barrier, peers)


def transfer(source, landing, sends, receives, slot, device):
    return pltpu.make_async_remote_copy(
        src_ref=source,
        dst_ref=landing,
        send_sem=sends.at[slot],
        recv_sem=receives.at[slot],
        device_id=device,
        device_id_type=pl.DeviceIdType.MESH,
    )


def half_slot(down, right):
    return (0 if down < 0 else 1) + (0 if right < 0 else 8)


def halo_copies(source, ext, sends, receives):
    def row_copy(down, right, device):
        return transfer(
            source(down, right),
            ext.at[:, own_block(right), zone(-down), :],
            sends,
            receives,
            half_slot(down, right),
            device,
        )

    def col_copy(right, device):
        at = SIDES.index((0, right))
        return transfer(
            source(0, right),
            ext.at[:, rim_block(-right), zone(0), :],
            sends,
            receives,
            at,
            device,
        )

    def corner_copy(down, right, device):
        at = SIDES.index((down, right))
        return transfer(
            ext.at[:, own_block(right), zone(-down), :],
            ext.at[:, rim_block(-right), zone(-down), :],
            sends,
            receives,
            at,
            device,
        )

    return row_copy, col_copy, corner_copy


def halo_begin(copies, row, col):
    row_copy, col_copy, _ = copies
    for down, right in CORNERS:

        @pl.when(inside(row + down, col))
        def _():
            row_copy(down, right, (row + down, col)).start()

    for right in (-1, 1):

        @pl.when(inside(row, col + right))
        def _():
            col_copy(right, (row, col + right)).start()


def blank_outside(ext, row, col):
    for down, right in SIDES:

        @pl.when(jnp.logical_not(inside(row - down, col - right)))
        def _():
            blocks = slice(1, 3) if right == 0 else slice(rim_block(-right), rim_block(-right) + 1)
            part = ext.at[:, blocks, zone(-down), :]
            part[...] = jnp.zeros(part.shape, jnp.float32)


def halo_finish(copies, row, col):
    row_copy, col_copy, corner_copy = copies
    for down, right in CORNERS:

        @pl.when(inside(row - down, col))
        def _():
            row_copy(down, right, (row - down, col)).wait_recv()

        @pl.when(inside(row - down, col) & inside(row, col + right))
        def _():
            corner_copy(down, right, (row, col + right)).start()

    for right in (-1, 1):

        @pl.when(inside(row, col - right))
        def _():
            col_copy(right, (row, col - right)).wait_recv()

    for down, right in CORNERS:

        @pl.when(inside(row - down, col - right))
        def _():
            corner_copy(down, right, (row, col - right)).wait_recv()

    for down, right in CORNERS:

        @pl.when(inside(row + down, col))
        def _():
            row_copy(down, right, (row + down, col)).wait_send()

        @pl.when(inside(row - down, col) & inside(row, col + right))
        def _():
            corner_copy(down, right, (row, col + right)).wait_send()

    for right in (-1, 1):

        @pl.when(inside(row, col + right))
        def _():
            col_copy(right, (row, col + right)).wait_send()


def prepare(offs, probe, amps, order, turned, sorted_amps, swap):
    lane = lax.broadcasted_iota(jnp.int32, (CHUNK, LANES), 1)

    def one_slot(slot, carry):
        left = offs[1, slot] % TILE
        shift = left % LANES
        low = jnp.where(lane >= shift, 1, 0)
        straight = low != left // LANES
        for p in range(2):
            for at in range(0, TILE, CHUNK):
                rows = slice(at, at + CHUNK)
                a = pltpu.roll(probe[p, rows, :LANES], shift, 1)
                b = pltpu.roll(probe[p, rows, LANES:], shift, 1)
                turned[slot, p, 0, rows, :] = jnp.where(straight, a, b)
                turned[slot, p, 1, rows, :] = jnp.where(straight, b, a)
        swap[...] = jnp.dot(order[0], amps[slot], preferred_element_type=jnp.float32).astype(jnp.bfloat16)
        placed = jnp.dot(swap[...], order[1], preferred_element_type=jnp.float32).astype(jnp.bfloat16)
        sorted_amps[slot, 0] = placed[:, :LANES]
        sorted_amps[slot, 1] = placed[:, LANES:]
        return carry

    lax.fori_loop(0, MAXPOS, one_slot, 0)


def halo_kernel(
    offs_in, field, probe_in, amps_in, order_in, ext, turned, sorted_amps,
    offs, probe, amps, order, swap, loads, sends, receives,
):
    row, col = lax.axis_index("row"), lax.axis_index("col")
    staged = [
        pltpu.make_async_copy(there, here, loads.at[at])
        for at, (there, here) in enumerate(
            [(offs_in, offs), (probe_in, probe), (order_in, order), (amps_in, amps)]
            + [
                (field.at[:, :, b * LANES : (b + 1) * LANES], ext.at[:, 1 + b, zone(0), :])
                for b in range(2)
            ]
        )
    ]
    for load in staged:
        load.start()
    greet(row, col)

    def source(down, right):
        cols = slice(0, LANES) if right < 0 else slice(LANES, 2 * LANES)
        return field.at[:, edge(down, TILE), cols]

    copies = halo_copies(source, ext, sends, receives)
    halo_begin(copies, row, col)
    blank_outside(ext, row, col)
    for load in staged:
        load.wait()
    prepare(offs, probe, amps, order, turned, sorted_amps, swap)
    halo_finish(copies, row, col)


def gradient_kernel(planes, offs, cnt, ext, turned, amps, mats, canvas, *scratch):
    canvas[...] = jnp.zeros_like(canvas)
    lane = lax.broadcasted_iota(jnp.int32, (CHUNK, LANES), 1)
    bf16 = jnp.bfloat16

    def product(a, b):
        return jnp.dot(a, b, preferred_element_type=jnp.float32)

    def stages(slot, used, buffers):
        waves, halves, spectra = buffers
        top = offs[0, slot]
        left = offs[1, slot]
        near = [lane >= left - b * LANES for b in range(2)]

        def gather():
            for at in range(0, HALF, CHUNK):
                for b in range(2):
                    cols = slice(b * LANES, (b + 1) * LANES)
                    parts = []
                    for far in (0, HALF):
                        rows = pl.ds(top + at + far, CHUNK)
                        wr, wi = [
                            jnp.where(near[b], ext[p, b, rows, :], ext[p, b + 2, rows, :])
                            for p in range(2)
                        ]
                        pr = turned[slot, 0, b, at + far : at + far + CHUNK, :]
                        pi = turned[slot, 1, b, at + far : at + far + CHUNK, :]
                        parts.append((pr * wr - pi * wi, pr * wi + pi * wr))
                    for p in range(2):
                        rows = slice(p * HALF + at, p * HALF + at + CHUNK)
                        waves[0, rows, cols] = (parts[0][p] + parts[1][p]).astype(bf16)
                        waves[1, rows, cols] = (parts[0][p] - parts[1][p]).astype(bf16)

        def forward_rows():
            for parity in range(2):
                y = product(mats[parity], waves[parity])
                a, b = y[:, :LANES], y[:, LANES:]
                rows = slice(parity * HALF, (parity + 1) * HALF)
                for at, z in enumerate((a + b, a - b)):
                    halves[at, rows, :LANES] = z[:HALF].astype(bf16)
                    halves[at, rows, LANES:] = z[HALF:].astype(bf16)

        def forward_cols():
            for parity in range(2):
                spectra[parity] = product(halves[parity], mats[2 + parity])

        def residual():
            for parity in range(2):
                for at in range(0, TILE, CHUNK):
                    sr = spectra[parity, at : at + CHUNK, :LANES]
                    si = spectra[parity, at : at + CHUNK, LANES:]
                    amp = amps[slot, parity, at : at + CHUNK, :].astype(jnp.float32)
                    factor = 1.0 - amp * lax.rsqrt(sr * sr + si * si + smooth_term)
                    if used is not None:
                        factor = jnp.where(used, factor, 0.0)
                    odd, inner = divmod(at, HALF)
                    cols = slice(parity * LANES, (parity + 1) * LANES)
                    waves[odd, inner : inner + CHUNK, cols] = (sr * factor).astype(bf16)
                    waves[odd, HALF + inner : HALF + inner + CHUNK, cols] = (si * factor).astype(bf16)

        def back_rows():
            e = product(mats[2], waves[0])
            o = product(mats[3], waves[1])
            for at, z in enumerate((e + o, e - o)):
                rows = slice(at * HALF, (at + 1) * HALF)
                for parity in range(2):
                    cols = slice(parity * LANES, (parity + 1) * LANES)
                    halves[parity, rows, :LANES] = z[:HALF, cols].astype(bf16)
                    halves[parity, rows, LANES:] = z[HALF:, cols].astype(bf16)

        def back_cols():
            for parity in range(2):
                spectra[parity] = product(halves[parity], mats[parity])

        def scatter():
            for at in range(0, TILE, CHUNK):
                rows = pl.ds(top + at, CHUNK)
                er, ei = [spectra[0, at : at + CHUNK, p * LANES : (p + 1) * LANES] for p in range(2)]
                pr_, pi_ = [spectra[1, at : at + CHUNK, p * LANES : (p + 1) * LANES] for p in range(2)]
                for b in range(2):
                    br, bi = (er + pr_, ei + pi_) if b == 0 else (er - pr_, ei - pi_)
                    pr = turned[slot, 0, b, at : at + CHUNK, :]
                    pi = turned[slot, 1, b, at : at + CHUNK, :]
                    pieces = [pr * br + pi * bi, pr * bi - pi * br]
                    if planes > 2:
                        light = pr * pr + pi * pi
                        pieces.append(light if used is None else jnp.where(used, light, 0.0))
                    for p, piece in enumerate(pieces):
                        canvas[p, b, rows, :] += jnp.where(near[b], piece, 0.0)
                        canvas[p, b + 2, rows, :] += jnp.where(near[b], 0.0, piece)

        return [gather, forward_rows, forward_cols, residual, back_rows, back_cols, scatter]

    first, second = scratch[:3], scratch[3:]

    def two_slots(pair, carry):
        a = stages(2 * pair, None, first)
        b = stages(2 * pair + 1, 2 * pair + 1 < cnt[0], second)
        a[0]()
        for at in range(1, len(a)):
            a[at]()
            b[at - 1]()
        b[-1]()
        return carry

    lax.fori_loop(0, (cnt[0] + 1) // 2, two_slots, 0)


def update_kernel(first, canvas, ext, *refs):
    if first:
        new, scale_out = refs[:2]
        halo_sems = refs[-2:]
        refs = refs[2:-2]
    else:
        scale_in, new = refs[:2]
        refs = refs[2:]
    land_corner, land_col, land_row, total, sends, receives = refs
    row, col = lax.axis_index("row"), lax.axis_index("col")
    greet(row, col)

    def corner_copy(down, right, device):
        at = SIDES.index((down, right))
        return transfer(
            canvas.at[:, rim_block(right), zone(down), :],
            land_corner.at[at - 4],
            sends,
            receives,
            at,
            device,
        )

    def col_copy(right, device):
        at = SIDES.index((0, right))
        return transfer(
            canvas.at[:, rim_block(right), zone(0), :], land_col.at[at - 2], sends, receives, at, device
        )

    def row_copy(down, right, device):
        vertical = 0 if down < 0 else 1
        return transfer(
            total.at[:, own_block(right) - 1, zone(down), :],
            land_row.at[vertical, :, own_block(right) - 1],
            sends,
            receives,
            half_slot(down, right),
            device,
        )

    for down, right in CORNERS:

        @pl.when(inside(row + down, col + right))
        def _():
            corner_copy(down, right, (row, col + right)).start()

    for right in (-1, 1):

        @pl.when(inside(row, col + right))
        def _():
            col_copy(right, (row, col + right)).start()

    total[...] = canvas[:, 1:3]

    def send_half(side):
        block = own_block(side) - 1
        for down in (-1, 1):

            @pl.when(inside(row + down, col) & inside(row, col + side))
            def _():
                corner_copy(down, -side, (row, col + side)).wait_recv()
                total[:, block, zone(down), :] += land_corner[SIDES.index((down, -side)) - 4]

            @pl.when(inside(row + down, col))
            def _():
                row_copy(down, side, (row + down, col)).start()

    @pl.when(col % 2 == 1)
    def _():
        send_half(-1)
        send_half(1)

    @pl.when(col % 2 == 0)
    def _():
        send_half(1)
        send_half(-1)

    for right in (-1, 1):

        @pl.when(inside(row, col - right))
        def _():
            col_copy(right, (row, col - right)).wait_recv()
            total[:, own_block(-right) - 1, zone(0), :] += land_col[SIDES.index((0, right)) - 2]

    for down, right in CORNERS:

        @pl.when(inside(row - down, col))
        def _():
            row_copy(down, right, (row - down, col)).wait_recv()
            part = slice(RIM, 2 * RIM) if down > 0 else slice(TILE, TILE + RIM)
            total[:, own_block(right) - 1, part, :] += land_row[0 if down < 0 else 1, :, own_block(right) - 1]

    for down, right in CORNERS:

        @pl.when(inside(row + down, col + right))
        def _():
            corner_copy(down, right, (row, col + right)).wait_send()

        @pl.when(inside(row + down, col))
        def _():
            row_copy(down, right, (row + down, col)).wait_send()

    for right in (-1, 1):

        @pl.when(inside(row, col + right))
        def _():
            col_copy(right, (row, col + right)).wait_send()

    for block in range(2):
        if first:
            scale = step_size / (total[2, block, zone(0), :] + regular_term)
            scale_out[block] = scale
        else:
            scale = scale_in[block]
        for p in range(2):
            value = ext[p, 1 + block, zone(0), :] - total[p, block, zone(0), :] * scale
            if first:
                new[p, 1 + block, zone(0), :] = value
            else:
                new[p, :, block * LANES : (block + 1) * LANES] = value

    if first:

        def source(down, right):
            part = {-1: slice(RIM, 2 * RIM), 0: zone(0), 1: slice(TILE, TILE + RIM)}[down]
            return new.at[:, own_block(right), part, :]

        copies = halo_copies(source, new, *halo_sems)
        halo_begin(copies, row, col)
        blank_outside(new, row, col)
        halo_finish(copies, row, col)


def vmem(count):
    return [pl.BlockSpec(memory_space=pltpu.VMEM)] * count


def smem(count):
    return [pl.BlockSpec(memory_space=pltpu.SMEM)] * count


def dma_sems():
    return [pltpu.SemaphoreType.DMA((10,))] * 2


def f32(*shape):
    return jax.ShapeDtypeStruct(shape, jnp.float32)


def wire_params(identity):
    return pltpu.CompilerParams(
        collective_id=identity, has_side_effects=True, vmem_limit_bytes=VMEM_LIMIT
    )


def gradient(planes, offs, cnt, ext, turned, amps, mats):
    slot_scratch = [
        pltpu.VMEM((2, TILE, TILE), jnp.bfloat16),
        pltpu.VMEM((2, TILE, TILE), jnp.bfloat16),
        pltpu.VMEM((2, TILE, TILE), jnp.float32),
    ]
    return pl.pallas_call(
        functools.partial(gradient_kernel, planes),
        out_shape=f32(planes, 4, 2 * TILE, LANES),
        in_specs=smem(2) + vmem(4),
        out_specs=vmem(1)[0],
        scratch_shapes=slot_scratch * 2,
        compiler_params=pltpu.CompilerParams(vmem_limit_bytes=VMEM_LIMIT),
        name=f"gradient{planes}",
    )(offs, cnt, ext, turned, amps, mats)


def halo(offs, field, probe, amps, order):
    return pl.pallas_call(
        halo_kernel,
        out_shape=[
            f32(2, 4, 2 * TILE, LANES),
            f32(MAXPOS, 2, 2, TILE, LANES),
            jax.ShapeDtypeStruct((MAXPOS, 2, TILE, LANES), jnp.bfloat16),
        ],
        in_specs=[pl.BlockSpec(memory_space=pltpu.HBM)] * 5,
        out_specs=vmem(3),
        scratch_shapes=[
            pltpu.SMEM((2, MAXPOS), jnp.int32),
            pltpu.VMEM((2, TILE, TILE), jnp.float32),
            pltpu.VMEM((MAXPOS, TILE, TILE), jnp.bfloat16),
            pltpu.VMEM((2, TILE, TILE), jnp.bfloat16),
            pltpu.VMEM((TILE, TILE), jnp.bfloat16),
            pltpu.SemaphoreType.DMA((6,)),
        ]
        + dma_sems(),
        compiler_params=wire_params(0),
        cost_estimate=WIRE_COST,
        name="halo",
    )(*[pltpu.with_memory_space_constraint(a, pltpu.HBM) for a in (offs, field, probe, amps, order)])


def update(planes, canvas, ext, scale):
    first = scale is None
    if first:
        shapes = [f32(2, 4, 2 * TILE, LANES), f32(2, TILE, LANES)]
    else:
        shapes = [f32(2, TILE, TILE)]
    operands = [canvas, ext] + ([] if first else [scale])
    return pl.pallas_call(
        functools.partial(update_kernel, first),
        out_shape=shapes,
        in_specs=vmem(len(operands)),
        out_specs=vmem(len(shapes)),
        scratch_shapes=[
            pltpu.VMEM((4, planes, HALF, LANES), jnp.float32),
            pltpu.VMEM((2, planes, TILE, LANES), jnp.float32),
            pltpu.VMEM((2, planes, 2, HALF, LANES), jnp.float32),
            pltpu.VMEM((planes, 2, 2 * TILE, LANES), jnp.float32),
        ]
        + dma_sems() * (2 if first else 1),
        compiler_params=wire_params(1 if first else 2),
        cost_estimate=WIRE_COST,
        name="exchange" if first else "finish",
    )(*operands)


def per_device(object_field, probe_field, amplitudes, offsets, counts):
    mats = jnp.asarray(dft_tables())
    order = jnp.asarray(order_table())
    offs = offsets.reshape(MAXPOS, 2).T
    cnt = counts.reshape(1)
    amps = amplitudes.reshape(MAXPOS, TILE, TILE)
    ext, turned, amps = halo(offs, object_field, probe_field, amps, order)
    scale = None
    for iteration in range(ITERS):
        planes = 3 if iteration == 0 else 2
        canvas = gradient(planes, offs, cnt, ext, turned, amps, mats)
        if iteration == 0:
            ext, scale = update(planes, canvas, ext, None)
        else:
            (field,) = update(planes, canvas, ext, scale)
    return field


def solution(mesh):
    in_specs = (
        P(None, "row", "col"),
        P(),
        P("row", "col", None, None, None),
        P("row", "col", None, None),
        P("row", "col"),
    )
    out_specs = P(None, "row", "col")
    return jax.shard_map(
        per_device, mesh=mesh, in_specs=in_specs, out_specs=out_specs, check_vma=False
    )
```

```python
import functools
import math

import jax
import jax.numpy as jnp
import numpy as np
from jax import lax
from jax.experimental import pallas as pl
from jax.experimental.pallas import tpu as pltpu
from jax.sharding import PartitionSpec as P

TILE = 256
RIM = 128
MAXPOS = 6
ITERS = 2
LANES = 128
HALF = 128
CHUNK = 32
VMEM_LIMIT = 28 * 1024 * 1024
WIRE_COST = pl.CostEstimate(flops=0, transcendentals=0, bytes_accessed=40_000_000)

smooth_term = 0.25
step_size = 0.5
regular_term = 1.0

AXES = ("row", "col")
SIDES = [(-1, 0), (1, 0), (0, -1), (0, 1), (-1, -1), (-1, 1), (1, -1), (1, 1)]
CORNERS = SIDES[4:]


def dft_tables():
    positions = np.arange(TILE)
    phase_step = (positions[:, None] * positions[None, :]) % TILE
    angle = phase_step.astype(np.float32) * np.float32(2.0 * math.pi / TILE)
    scale = np.float32(1.0 / math.sqrt(TILE))
    real = np.cos(angle).astype(np.float32) * scale
    imag = -np.sin(angle).astype(np.float32) * scale
    left, right = [], []
    for parity in range(2):
        r = real[parity::2, :HALF]
        i = imag[parity::2, :HALF]
        m = np.block([[r, -i], [i, r]])
        left.append(m)
        right.append(m.T)
    return np.stack(left + right).astype(jnp.bfloat16)


def order_table():
    picked = np.concatenate([np.arange(0, TILE, 2), np.arange(1, TILE, 2)])
    table = np.zeros((TILE, TILE), np.float32)
    table[np.arange(TILE), picked] = 1.0
    return np.stack([table, table.T]).astype(jnp.bfloat16)


def edge(step, length):
    if step < 0:
        return slice(0, RIM)
    if step > 0:
        return slice(length - RIM, length)
    return slice(0, length)


def zone(step):
    return (slice(0, RIM), slice(RIM, RIM + TILE), slice(RIM + TILE, 2 * RIM + TILE))[step + 1]


def own_rows(down):
    return slice(RIM, 2 * RIM) if down < 0 else slice(TILE, TILE + RIM)


def rim_block(right):
    return 0 if right < 0 else 3


def own_block(right):
    return 1 if right < 0 else 2


def inside(row, col):
    rows, cols = lax.axis_size("row"), lax.axis_size("col")
    return (row >= 0) & (row < rows) & (col >= 0) & (col < cols)


def greet(row, col):
    barrier = pltpu.get_barrier_semaphore()
    peers = 0
    for down, right in SIDES[:4]:
        present = inside(row + down, col + right)
        peers = peers + jnp.where(present, 1, 0)

        @pl.when(present)
        def _():
            pl.semaphore_signal(
                barrier,
                inc=1,
                device_id=(row + down, col + right),
                device_id_type=pl.DeviceIdType.MESH,
            )

    pl.semaphore_wait(barrier, peers)


def transfer(source, landing, sends, receives, slot, device):
    return pltpu.make_async_remote_copy(
        src_ref=source,
        dst_ref=landing,
        send_sem=sends.at[slot],
        recv_sem=receives.at[slot],
        device_id=device,
        device_id_type=pl.DeviceIdType.MESH,
    )


def half_slot(down, right):
    return (0 if down < 0 else 1) + (0 if right < 0 else 8)


def halo_copies(source, ext, sends, receives):
    def row_copy(down, right, device):
        return transfer(
            source(down, right),
            ext.at[:, own_block(right), zone(-down), :],
            sends,
            receives,
            half_slot(down, right),
            device,
        )

    def col_copy(down, right, device):
        at = SIDES.index((0, right)) + (0 if down < 0 else 8)
        return transfer(
            source(down, right),
            ext.at[:, rim_block(-right), own_rows(down), :],
            sends,
            receives,
            at,
            device,
        )

    def corner_copy(down, right, device):
        at = SIDES.index((down, right))
        return transfer(
            ext.at[:, own_block(right), zone(-down), :],
            ext.at[:, rim_block(-right), zone(-down), :],
            sends,
            receives,
            at,
            device,
        )

    return row_copy, col_copy, corner_copy


def start_rows(copies, down, row, col):
    for right in (-1, 1):

        @pl.when(inside(row + down, col))
        def _():
            copies[0](down, right, (row + down, col)).start()


def start_cols(copies, down, row, col):
    for right in (-1, 1):

        @pl.when(inside(row, col + right))
        def _():
            copies[1](down, right, (row, col + right)).start()


def blank_outside(ext, row, col):
    for down, right in SIDES:

        @pl.when(jnp.logical_not(inside(row - down, col - right)))
        def _():
            blocks = slice(1, 3) if right == 0 else slice(rim_block(-right), rim_block(-right) + 1)
            part = ext.at[:, blocks, zone(-down), :]
            part[...] = jnp.zeros(part.shape, jnp.float32)


def halo_finish(copies, row, col):
    row_copy, col_copy, corner_copy = copies
    for down, right in CORNERS:

        @pl.when(inside(row - down, col))
        def _():
            row_copy(down, right, (row - down, col)).wait_recv()

        @pl.when(inside(row - down, col) & inside(row, col + right))
        def _():
            corner_copy(down, right, (row, col + right)).start()

    for down, right in CORNERS:

        @pl.when(inside(row, col - right))
        def _():
            col_copy(down, right, (row, col - right)).wait_recv()

    for down, right in CORNERS:

        @pl.when(inside(row - down, col - right))
        def _():
            corner_copy(down, right, (row, col - right)).wait_recv()

    for down, right in CORNERS:

        @pl.when(inside(row + down, col))
        def _():
            row_copy(down, right, (row + down, col)).wait_send()

        @pl.when(inside(row - down, col) & inside(row, col + right))
        def _():
            corner_copy(down, right, (row, col + right)).wait_send()

    for down, right in CORNERS:

        @pl.when(inside(row, col + right))
        def _():
            col_copy(down, right, (row, col + right)).wait_send()


def prepare(offs, probe, amps, order, turned, sorted_amps, swap):
    lane = lax.broadcasted_iota(jnp.int32, (CHUNK, LANES), 1)

    def one_slot(slot, carry):
        left = offs[1, slot] % TILE
        shift = left % LANES
        low = jnp.where(lane >= shift, 1, 0)
        straight = low != left // LANES
        for p in range(2):
            for at in range(0, TILE, CHUNK):
                rows = slice(at, at + CHUNK)
                a = pltpu.roll(probe[p, rows, :LANES], shift, 1)
                b = pltpu.roll(probe[p, rows, LANES:], shift, 1)
                turned[slot, p, 0, rows, :] = jnp.where(straight, a, b)
                turned[slot, p, 1, rows, :] = jnp.where(straight, b, a)
        swap[...] = jnp.dot(order[0], amps[slot], preferred_element_type=jnp.float32).astype(jnp.bfloat16)
        placed = jnp.dot(swap[...], order[1], preferred_element_type=jnp.float32).astype(jnp.bfloat16)
        sorted_amps[slot, 0] = placed[:, :LANES]
        sorted_amps[slot, 1] = placed[:, LANES:]
        return carry

    lax.fori_loop(0, MAXPOS, one_slot, 0)


def halo_kernel(
    offs_in, field, probe_in, amps_in, order_in, ext, turned, sorted_amps,
    offs, probe, amps, order, swap, loads, sends, receives,
):
    row, col = lax.axis_index("row"), lax.axis_index("col")
    staged = [
        pltpu.make_async_copy(there, here, loads.at[at])
        for at, (there, here) in enumerate(
            [(offs_in, offs), (probe_in, probe), (order_in, order), (amps_in, amps)]
            + [
                (field.at[:, :, b * LANES : (b + 1) * LANES], ext.at[:, 1 + b, zone(0), :])
                for b in range(2)
            ]
        )
    ]
    for load in staged:
        load.start()
    greet(row, col)

    def source(down, right):
        cols = slice(0, LANES) if right < 0 else slice(LANES, 2 * LANES)
        return field.at[:, edge(down, TILE), cols]

    copies = halo_copies(source, ext, sends, receives)
    for down in (-1, 1):
        start_rows(copies, down, row, col)
    for down in (-1, 1):
        start_cols(copies, down, row, col)
    blank_outside(ext, row, col)
    for load in staged:
        load.wait()
    prepare(offs, probe, amps, order, turned, sorted_amps, swap)
    halo_finish(copies, row, col)


def gradient_kernel(planes, offs, cnt, ext, turned, amps, mats, canvas, *scratch):
    canvas[...] = jnp.zeros_like(canvas)
    lane = lax.broadcasted_iota(jnp.int32, (CHUNK, LANES), 1)
    bf16 = jnp.bfloat16

    def product(a, b):
        return jnp.dot(a, b, preferred_element_type=jnp.float32)

    def stages(slot, used, buffers):
        waves, halves, spectra = buffers
        top = offs[0, slot]
        left = offs[1, slot]
        near = [lane >= left - b * LANES for b in range(2)]

        def gather():
            for at in range(0, HALF, CHUNK):
                for b in range(2):
                    cols = slice(b * LANES, (b + 1) * LANES)
                    parts = []
                    for far in (0, HALF):
                        rows = pl.ds(top + at + far, CHUNK)
                        wr, wi = [
                            jnp.where(near[b], ext[p, b, rows, :], ext[p, b + 2, rows, :])
                            for p in range(2)
                        ]
                        pr = turned[slot, 0, b, at + far : at + far + CHUNK, :]
                        pi = turned[slot, 1, b, at + far : at + far + CHUNK, :]
                        parts.append((pr * wr - pi * wi, pr * wi + pi * wr))
                    for p in range(2):
                        rows = slice(p * HALF + at, p * HALF + at + CHUNK)
                        waves[0, rows, cols] = (parts[0][p] + parts[1][p]).astype(bf16)
                        waves[1, rows, cols] = (parts[0][p] - parts[1][p]).astype(bf16)

        def forward_rows():
            for parity in range(2):
                y = product(mats[parity], waves[parity])
                a, b = y[:, :LANES], y[:, LANES:]
                rows = slice(parity * HALF, (parity + 1) * HALF)
                for at, z in enumerate((a + b, a - b)):
                    halves[at, rows, :LANES] = z[:HALF].astype(bf16)
                    halves[at, rows, LANES:] = z[HALF:].astype(bf16)

        def forward_cols():
            for parity in range(2):
                spectra[parity] = product(halves[parity], mats[2 + parity])

        def residual():
            for parity in range(2):
                for at in range(0, TILE, CHUNK):
                    sr = spectra[parity, at : at + CHUNK, :LANES]
                    si = spectra[parity, at : at + CHUNK, LANES:]
                    amp = amps[slot, parity, at : at + CHUNK, :].astype(jnp.float32)
                    factor = 1.0 - amp * lax.rsqrt(sr * sr + si * si + smooth_term)
                    if used is not None:
                        factor = jnp.where(used, factor, 0.0)
                    odd, inner = divmod(at, HALF)
                    cols = slice(parity * LANES, (parity + 1) * LANES)
                    waves[odd, inner : inner + CHUNK, cols] = (sr * factor).astype(bf16)
                    waves[odd, HALF + inner : HALF + inner + CHUNK, cols] = (si * factor).astype(bf16)

        def back_rows():
            e = product(mats[2], waves[0])
            o = product(mats[3], waves[1])
            for at, z in enumerate((e + o, e - o)):
                rows = slice(at * HALF, (at + 1) * HALF)
                for parity in range(2):
                    cols = slice(parity * LANES, (parity + 1) * LANES)
                    halves[parity, rows, :LANES] = z[:HALF, cols].astype(bf16)
                    halves[parity, rows, LANES:] = z[HALF:, cols].astype(bf16)

        def back_cols():
            for parity in range(2):
                spectra[parity] = product(halves[parity], mats[parity])

        def scatter():
            for at in range(0, TILE, CHUNK):
                rows = pl.ds(top + at, CHUNK)
                er, ei = [spectra[0, at : at + CHUNK, p * LANES : (p + 1) * LANES] for p in range(2)]
                pr_, pi_ = [spectra[1, at : at + CHUNK, p * LANES : (p + 1) * LANES] for p in range(2)]
                for b in range(2):
                    br, bi = (er + pr_, ei + pi_) if b == 0 else (er - pr_, ei - pi_)
                    pr = turned[slot, 0, b, at : at + CHUNK, :]
                    pi = turned[slot, 1, b, at : at + CHUNK, :]
                    pieces = [pr * br + pi * bi, pr * bi - pi * br]
                    if planes > 2:
                        light = pr * pr + pi * pi
                        pieces.append(light if used is None else jnp.where(used, light, 0.0))
                    for p, piece in enumerate(pieces):
                        canvas[p, b, rows, :] += jnp.where(near[b], piece, 0.0)
                        canvas[p, b + 2, rows, :] += jnp.where(near[b], 0.0, piece)

        return [gather, forward_rows, forward_cols, residual, back_rows, back_cols, scatter]

    first, second = scratch[:3], scratch[3:]

    def two_slots(pair, carry):
        a = stages(2 * pair, None, first)
        b = stages(2 * pair + 1, 2 * pair + 1 < cnt[0], second)
        a[0]()
        for at in range(1, len(a)):
            a[at]()
            b[at - 1]()
        b[-1]()
        return carry

    lax.fori_loop(0, (cnt[0] + 1) // 2, two_slots, 0)


def update_kernel(first, canvas, ext, *refs):
    if first:
        new, scale_out = refs[:2]
        halo_sems = refs[-2:]
        refs = refs[2:-2]
    else:
        scale_in, new = refs[:2]
        refs = refs[2:]
    land_corner, land_col, land_row, total, sends, receives = refs
    row, col = lax.axis_index("row"), lax.axis_index("col")
    greet(row, col)

    def corner_copy(down, right, device):
        at = SIDES.index((down, right))
        return transfer(
            canvas.at[:, rim_block(right), zone(down), :],
            land_corner.at[at - 4],
            sends,
            receives,
            at,
            device,
        )

    def col_copy(right, device):
        at = SIDES.index((0, right))
        return transfer(
            canvas.at[:, rim_block(right), zone(0), :], land_col.at[at - 2], sends, receives, at, device
        )

    def row_copy(down, right, device):
        vertical = 0 if down < 0 else 1
        return transfer(
            total.at[:, own_block(right) - 1, zone(down), :],
            land_row.at[vertical, :, own_block(right) - 1],
            sends,
            receives,
            half_slot(down, right),
            device,
        )

    for down, right in CORNERS:

        @pl.when(inside(row + down, col + right))
        def _():
            corner_copy(down, right, (row, col + right)).start()

    for right in (-1, 1):

        @pl.when(inside(row, col + right))
        def _():
            col_copy(right, (row, col + right)).start()

    total[...] = canvas[:, 1:3]

    def send_half(side):
        block = own_block(side) - 1
        for down in (-1, 1):

            @pl.when(inside(row + down, col) & inside(row, col + side))
            def _():
                corner_copy(down, -side, (row, col + side)).wait_recv()
                total[:, block, zone(down), :] += land_corner[SIDES.index((down, -side)) - 4]

            @pl.when(inside(row + down, col))
            def _():
                row_copy(down, side, (row + down, col)).start()

    @pl.when(col % 2 == 1)
    def _():
        send_half(-1)
        send_half(1)

    @pl.when(col % 2 == 0)
    def _():
        send_half(1)
        send_half(-1)

    for right in (-1, 1):

        @pl.when(inside(row, col - right))
        def _():
            col_copy(right, (row, col - right)).wait_recv()
            total[:, own_block(-right) - 1, zone(0), :] += land_col[SIDES.index((0, right)) - 2]

    def apply(down):
        part = own_rows(down)
        kept = slice(part.start - RIM, part.stop - RIM)
        for block in range(2):
            if first:
                scale = step_size / (total[2, block, part, :] + regular_term)
                scale_out[block, kept] = scale
            else:
                scale = scale_in[block, kept]
            for p in range(2):
                value = ext[p, 1 + block, part, :] - total[p, block, part, :] * scale
                if first:
                    new[p, 1 + block, part, :] = value
                else:
                    new[p, kept, block * LANES : (block + 1) * LANES] = value

    copies = None
    if first:

        def source(down, right):
            return new.at[:, own_block(right), own_rows(down), :]

        copies = halo_copies(source, new, *halo_sems)

    for down in (-1, 1):

        @pl.when(jnp.logical_not(inside(row + down, col)))
        def _():
            apply(down)
            if first:
                start_cols(copies, down, row, col)

    if first:
        blank_outside(new, row, col)

    for down in (-1, 1):

        @pl.when(inside(row + down, col))
        def _():
            for right in (-1, 1):
                row_copy(-down, right, (row + down, col)).wait_recv()
                total[:, own_block(right) - 1, own_rows(down), :] += land_row[
                    0 if down > 0 else 1, :, own_block(right) - 1
                ]
            apply(down)
            if first:
                start_rows(copies, down, row, col)
                start_cols(copies, down, row, col)

    if first:
        halo_finish(copies, row, col)

    for down, right in CORNERS:

        @pl.when(inside(row + down, col + right))
        def _():
            corner_copy(down, right, (row, col + right)).wait_send()

        @pl.when(inside(row + down, col))
        def _():
            row_copy(down, right, (row + down, col)).wait_send()

    for right in (-1, 1):

        @pl.when(inside(row, col + right))
        def _():
            col_copy(right, (row, col + right)).wait_send()


def vmem(count):
    return [pl.BlockSpec(memory_space=pltpu.VMEM)] * count


def smem(count):
    return [pl.BlockSpec(memory_space=pltpu.SMEM)] * count


def dma_sems():
    return [pltpu.SemaphoreType.DMA((12,))] * 2


def f32(*shape):
    return jax.ShapeDtypeStruct(shape, jnp.float32)


def wire_params(identity):
    return pltpu.CompilerParams(
        collective_id=identity, has_side_effects=True, vmem_limit_bytes=VMEM_LIMIT
    )


def gradient(planes, offs, cnt, ext, turned, amps, mats):
    slot_scratch = [
        pltpu.VMEM((2, TILE, TILE), jnp.bfloat16),
        pltpu.VMEM((2, TILE, TILE), jnp.bfloat16),
        pltpu.VMEM((2, TILE, TILE), jnp.float32),
    ]
    return pl.pallas_call(
        functools.partial(gradient_kernel, planes),
        out_shape=f32(planes, 4, 2 * TILE, LANES),
        in_specs=smem(2) + vmem(4),
        out_specs=vmem(1)[0],
        scratch_shapes=slot_scratch * 2,
        compiler_params=pltpu.CompilerParams(vmem_limit_bytes=VMEM_LIMIT),
        name=f"gradient{planes}",
    )(offs, cnt, ext, turned, amps, mats)


def halo(offs, field, probe, amps, order):
    return pl.pallas_call(
        halo_kernel,
        out_shape=[
            f32(2, 4, 2 * TILE, LANES),
            f32(MAXPOS, 2, 2, TILE, LANES),
            jax.ShapeDtypeStruct((MAXPOS, 2, TILE, LANES), jnp.bfloat16),
        ],
        in_specs=[pl.BlockSpec(memory_space=pltpu.HBM)] * 5,
        out_specs=vmem(3),
        scratch_shapes=[
            pltpu.SMEM((2, MAXPOS), jnp.int32),
            pltpu.VMEM((2, TILE, TILE), jnp.float32),
            pltpu.VMEM((MAXPOS, TILE, TILE), jnp.bfloat16),
            pltpu.VMEM((2, TILE, TILE), jnp.bfloat16),
            pltpu.VMEM((TILE, TILE), jnp.bfloat16),
            pltpu.SemaphoreType.DMA((6,)),
        ]
        + dma_sems(),
        compiler_params=wire_params(0),
        cost_estimate=WIRE_COST,
        name="halo",
    )(*[pltpu.with_memory_space_constraint(a, pltpu.HBM) for a in (offs, field, probe, amps, order)])


def update(planes, canvas, ext, scale):
    first = scale is None
    if first:
        shapes = [f32(2, 4, 2 * TILE, LANES), f32(2, TILE, LANES)]
    else:
        shapes = [f32(2, TILE, TILE)]
    operands = [canvas, ext] + ([] if first else [scale])
    return pl.pallas_call(
        functools.partial(update_kernel, first),
        out_shape=shapes,
        in_specs=vmem(len(operands)),
        out_specs=vmem(len(shapes)),
        scratch_shapes=[
            pltpu.VMEM((4, planes, HALF, LANES), jnp.float32),
            pltpu.VMEM((2, planes, TILE, LANES), jnp.float32),
            pltpu.VMEM((2, planes, 2, HALF, LANES), jnp.float32),
            pltpu.VMEM((planes, 2, 2 * TILE, LANES), jnp.float32),
        ]
        + dma_sems() * (2 if first else 1),
        compiler_params=wire_params(1 if first else 2),
        cost_estimate=WIRE_COST,
        name="exchange" if first else "finish",
    )(*operands)


def per_device(object_field, probe_field, amplitudes, offsets, counts):
    mats = jnp.asarray(dft_tables())
    order = jnp.asarray(order_table())
    offs = offsets.reshape(MAXPOS, 2).T
    cnt = counts.reshape(1)
    amps = amplitudes.reshape(MAXPOS, TILE, TILE)
    ext, turned, amps = halo(offs, object_field, probe_field, amps, order)
    scale = None
    for iteration in range(ITERS):
        planes = 3 if iteration == 0 else 2
        canvas = gradient(planes, offs, cnt, ext, turned, amps, mats)
        if iteration == 0:
            ext, scale = update(planes, canvas, ext, None)
        else:
            (field,) = update(planes, canvas, ext, scale)
    return field


def solution(mesh):
    in_specs = (
        P(None, "row", "col"),
        P(),
        P("row", "col", None, None, None),
        P("row", "col", None, None),
        P("row", "col"),
    )
    out_specs = P(None, "row", "col")
    return jax.shard_map(
        per_device, mesh=mesh, in_specs=in_specs, out_specs=out_specs, check_vma=False
    )
```
